32 devices in a mesh: samp: 8 (over y, x, core), feat: 4 (over z).
Axes of the slice: x: 2, y: 2, z: 4, core: 2. Of those that a mesh axis runs over, the one named last changes fastest.
Arguments:
- points: bfloat16 [4096, 128], P('samp'), may hold values from -6 to 6
- frequencies: bfloat16 [128, 16384], P(None, 'feat'), may hold values from -0.5 to 0.5
- phases: float32 [16384], P('feat'), may hold values from -3.140625 to 3.140625
- signs: int32 [4096], P('samp'), may hold values from -1 to 1, as said below
- picks: int32 [128], P('samp'), may hold values from 0 to 4095, as said below
Outputs:
- gram: float32 [16384, 16384], P('feat', 'samp')
The draws below stay inside these ranges and needn't reach their ends.
Inputs may be any that keep to these rules, and one draw needn't show every extreme that they name: `signs`: each entry is +1 or -1. `picks`: entry k names a row between (k // 16) * 512 and (k // 16 + 1) * 512 - 1; no row is named twice.
All inputs are finite; a program needn't handle non-finite values.
Results may differ from the reference program's by a relative error of at most 0.0009.
Values may be sent and summed in bfloat16 or wider, within the bound.
A program may use at most 128 MiB of HBM per device.

```python
import jax
import jax.numpy as jnp
from jax import lax

F = 16384
DIN = 128
ROWS_DEV = 512
KEEP_DEV = 16
NROWS = 4096
MROWS = 128
N_SAMP = 8
N_FEAT = 4


def draw_signs(key, part):
    coins = jax.random.randint(key, (NROWS,), 0, 2, dtype=jnp.int32)
    return (2 * coins - 1).astype(jnp.int32)


def draw_picks(key, part):
    groups = NROWS // ROWS_DEV
    keys = jax.random.split(jax.random.fold_in(key, 17), groups)
    orders = jax.vmap(lambda single: jax.random.permutation(single, ROWS_DEV))(keys)[:, :KEEP_DEV].astype(jnp.int32)
    group_ids = jnp.arange(groups, dtype=jnp.int32)
    first = orders[:, 0]
    target = jnp.where(group_ids == 0, 0, jnp.where(group_ids == groups - 1, ROWS_DEV - 1, first)).astype(jnp.int32)
    shift = target - first
    orders = jnp.remainder(orders + shift[:, None], ROWS_DEV).astype(jnp.int32)
    offsets = group_ids[:, None] * ROWS_DEV
    return (orders + offsets).reshape(-1).astype(jnp.int32)


def shard_levels(own_key, extent, shards, smallest, top_value):
    loudness = 1.0
    for dim, parts in shards:
        steps = jax.random.uniform(jax.random.fold_in(jax.random.fold_in(own_key, 6), dim), (parts,), jnp.float32, smallest / len(shards), top_value / len(shards))
        loudness = loudness * jnp.repeat(jnp.exp(steps), extent[dim] // parts).reshape((-1,) + (1,) * (len(extent) - 1 - dim))
    return loudness


def bell_draw(rng, dims, deviation, limit, cuts=(), held_as=jnp.bfloat16):
    result = jax.random.normal(rng, dims, jnp.float32) * deviation
    if len(cuts) > 0:
        result = shard_levels(rng, dims, cuts, -0.22, 0.18) * result
    return jnp.clip(result, min=-limit, max=limit).astype(held_as)


def setup_inputs(seed: int = 0) -> dict:
    splits = jax.random.split(jax.random.key(seed), 6)
    points = bell_draw(splits[0], (NROWS, DIN), 1.0, 6.0, ((0, 8),))
    frequencies = bell_draw(splits[1], (DIN, F), DIN ** -0.5, 0.5, ((1, 4),))
    phases = jnp.clip(jax.random.uniform(splits[2], (F,), jnp.float32, -3.140625, 3.140625), -3.140625, 3.140625)
    signs = draw_signs(jax.random.fold_in(splits[5], 71), 0)
    picks = draw_picks(jax.random.fold_in(splits[5], 71), 0)
    return dict(points=points, frequencies=frequencies, phases=phases, signs=signs, picks=picks)


def hadamard(order):
    table = jnp.ones((1, 1), jnp.float32)
    for level in range(order.bit_length() - 1):
        table = jnp.concatenate([jnp.concatenate([table, table], 1), jnp.concatenate([table, -table], 1)], 0)
    return table

def reference(points, frequencies, phases, signs, picks):
    blocks = N_FEAT
    width = F // blocks
    local_table = hadamard(ROWS_DEV)
    group_table = hadamard(N_SAMP)
    sign_values = signs.astype(jnp.float32)
    scale = 1.0 / float(MROWS * NROWS) ** 0.5
    freq_blocks = frequencies.reshape(DIN, blocks, width).transpose(1, 0, 2)
    phase_blocks = phases.reshape(blocks, width)

    def one_block(pair):
        freq_block, phase_block = pair
        phi = jnp.sqrt(jnp.float32(2.0)) * jnp.cos(jnp.dot(points, freq_block, preferred_element_type=jnp.float32) + phase_block[None, :])
        signed = phi * sign_values[:, None]
        shaped = signed.reshape(N_SAMP, ROWS_DEV, width)
        inner = jnp.einsum('jk,tkc->tjc', local_table, shaped, precision=lax.Precision.HIGHEST)
        outer = jnp.einsum('st,tjc->sjc', group_table, inner, precision=lax.Precision.HIGHEST)
        mixed = outer.reshape(NROWS, width)
        return (jnp.take(mixed, picks, axis=0) * scale).astype(jnp.bfloat16)
    pieces = lax.map(one_block, (freq_blocks, phase_blocks))
    sketch = pieces.transpose(1, 0, 2).reshape(MROWS, F)
    return lax.dot_general(sketch, sketch, (((0,), (0,)), ((), ())), preferred_element_type=jnp.float32)
```

```python
import functools

import jax
import jax.numpy as jnp
from jax import lax
from jax.experimental import pallas as pl
from jax.experimental.pallas import tpu as pltpu
from jax.sharding import PartitionSpec as P

MESH = pl.DeviceIdType.MESH
LANES = 128
SINE = (6.283185160089389, -41.34165503139731, 81.60100407217423, -76.54978227052618, 39.53670590280816)


def xor(a, b, bits):
    return sum(((a // 2**k + b // 2**k) % 2) * 2**k for k in range(bits))


def parity(value):
    for shift in (16, 8, 4, 2, 1):
        value = jnp.bitwise_xor(value, jnp.right_shift(value, shift))
    return jnp.bitwise_and(value, 1)


def flip(value):
    return 1.0 - 2.0 * parity(value).astype(jnp.float32)


def cosine(x):
    turns = x * 0.15915494309189535
    whole = (turns + 12582912.0) - 12582912.0
    y = 0.25 - jnp.abs(turns - whole)
    w = y * y
    p = w * SINE[4] + SINE[3]
    for c in SINE[2::-1]:
        p = p * w + c
    return p * y


def sketch_kernel(
    n, nf, scale, pts_ref, freq_ref, phase_ref, signs_ref, picks_ref, rows_ref, cols_ref,
    pts, sgn, pks, fbuf, pbuf, hloc, smat, acc,
    p_send, p_recv, p_fwd, s_send, s_recv, k_send, k_recv,
    r_send, r_recv, r_fwd, z_up, z_down, z_recv, local_sem,
):
    bits = n.bit_length() - 1
    me = lax.axis_index("samp")
    z = lax.axis_index("feat")
    core = me % 2
    mate = me + 1 - 2 * core
    rows = pts_ref.shape[0]
    fw = acc.shape[1]
    m = acc.shape[0]
    ratio = n // nf
    pieces = n // ratio
    root = me // ratio
    half = me % ratio

    loads = []
    if fw % LANES == 0:
        at = pl.multiple_of(me * fw, LANES)
        loads = [
            pltpu.make_async_copy(freq_ref.at[:, pl.ds(at, fw)], fbuf, local_sem.at[0]),
            pltpu.make_async_copy(phase_ref.at[:, pl.ds(at, fw)], pbuf, local_sem.at[1]),
        ]
    else:
        loads = [
            pltpu.make_async_copy(freq_ref, fbuf, local_sem.at[0]),
            pltpu.make_async_copy(phase_ref, pbuf, local_sem.at[1]),
        ]
    loads.append(pltpu.make_async_copy(pts_ref, pts.at[me], local_sem.at[2]))
    loads.append(pltpu.make_async_copy(signs_ref, sgn.at[me], local_sem.at[3]))
    loads.append(pltpu.make_async_copy(picks_ref, pks.at[me], local_sem.at[4]))
    for load in loads:
        load.start()

    barrier = pltpu.get_barrier_semaphore()
    for r in range(1, n):
        pl.semaphore_signal(barrier, inc=1, device_id={"samp": xor(me, r, bits)}, device_id_type=MESH)

    @pl.when(z + 1 < nf)
    def _():
        pl.semaphore_signal(barrier, inc=1, device_id={"feat": z + 1}, device_id_type=MESH)

    @pl.when(z > 0)
    def _():
        pl.semaphore_signal(barrier, inc=1, device_id={"feat": z - 1}, device_id_type=MESH)

    ends = jnp.where(z > 0, 1, 0) + jnp.where(z + 1 < nf, 1, 0)
    pl.semaphore_wait(barrier, n - 1 + ends)

    def remote(src, dst, send, recv, to):
        return pltpu.make_async_remote_copy(
            src_ref=src, dst_ref=dst, send_sem=send, recv_sem=recv, device_id=to, device_id_type=MESH
        )

    def small(r):
        peer = xor(me, r, bits)
        return (
            remote(picks_ref, pks.at[me], k_send.at[r], k_recv.at[me], {"samp": peer}),
            remote(signs_ref, sgn.at[me], s_send.at[r], s_recv.at[me], {"samp": peer}),
        )

    for r in range(1, n):
        for copy in small(r):
            copy.start()

    direct = [1] + list(range(2, n, 2))

    def own_points(r):
        return remote(pts_ref, pts.at[me], p_send.at[r], p_recv.at[me], {"samp": xor(me, r, bits)})

    for r in direct:
        own_points(r).start()

    def pass_points(src):
        return remote(pts.at[src], pts.at[src], p_fwd.at[src], p_recv.at[src], {"samp": mate})

    for load in loads:
        load.wait()
    for r in range(1, n):
        peer = xor(me, r, bits)
        remote(picks_ref, pks.at[peer], k_send.at[r], k_recv.at[peer], {"samp": peer}).wait_recv()

    picks = pks[...].reshape(m, LANES)
    lane = lax.broadcasted_iota(jnp.int32, (m, LANES), 1)
    for l in range(rows // LANES):
        hloc[:, l * LANES : (l + 1) * LANES] = flip(
            jnp.bitwise_and(jnp.bitwise_and(picks, rows - 1), lane + l * LANES)
        )
    acc[...] = jnp.zeros_like(acc)

    tile = min(rows, 256)

    def step(r, carry):
        src = xor(me, r, bits)

        @pl.when(r > 0)
        def _():
            remote(pts_ref, pts.at[src], p_send.at[r], p_recv.at[src], {"samp": mate}).wait_recv()
            remote(signs_ref, sgn.at[src], s_send.at[r], s_recv.at[src], {"samp": mate}).wait_recv()

        @pl.when(jnp.logical_and(r > 0, r % 2 == 0))
        def _():
            pass_points(src).start()

        group = flip(jnp.bitwise_and(pks[...].reshape(m, LANES), src * rows))
        for l in range(rows // LANES):
            s = slice(l * LANES, (l + 1) * LANES)
            smat[:, s] = (hloc[:, s] * (group * sgn[src, :, s].astype(jnp.float32))).astype(jnp.bfloat16)
        for k in range(rows // tile):
            s = slice(k * tile, (k + 1) * tile)
            x = jnp.dot(pts[src, s, :], fbuf[...], preferred_element_type=jnp.float32) + pbuf[...]
            c = cosine(x)
            hi = c.astype(jnp.bfloat16)
            lo = (c - hi.astype(jnp.float32)).astype(jnp.bfloat16)
            acc[...] += jnp.dot(smat[:, s], hi, preferred_element_type=jnp.float32) + jnp.dot(
                smat[:, s], lo, preferred_element_type=jnp.float32
            )
        return carry

    lax.fori_loop(0, n, step, 0)

    def part(g):
        return rows_ref.at[pl.ds(pl.multiple_of(g * fw, fw), fw), :]

    def slot(i):
        return cols_ref.at[pl.ds(pl.multiple_of(i * fw, fw), fw), :]

    rows_ref[pl.ds(pl.multiple_of(me * fw, fw), fw), :] = (acc[...] * scale).T.astype(jnp.bfloat16)

    def own_part(r):
        return remote(part(me), part(me), r_send.at[r], r_recv.at[me], {"samp": xor(me, r, bits)})

    for r in direct:
        own_part(r).start()

    def pass_part(src):
        return remote(part(src), part(src), r_fwd.at[src], r_recv.at[src], {"samp": mate})

    def up(src_ref, i):
        return remote(src_ref, slot(i), z_up.at[i], z_recv.at[i], {"feat": z + 1})

    def down(src_ref, i):
        return remote(src_ref, slot(i), z_down.at[i], z_recv.at[i], {"feat": z - 1})

    def exchange(r, carry):
        src = xor(me, r, bits)
        i = src % pieces

        @pl.when(r > 0)
        def _():
            remote(part(src), part(src), r_fwd.at[src], r_recv.at[src], {"samp": mate}).wait_recv()

        @pl.when(jnp.logical_and(r > 0, r % 2 == 0))
        def _():
            pass_part(src).start()

        mine = src // pieces == half

        @pl.when(jnp.logical_and(mine, z == root))
        def _():
            @pl.when(z + 1 < nf)
            def _():
                up(part(src), i).start()

            @pl.when(z > 0)
            def _():
                down(part(src), i).start()

            cols_ref[pl.ds(pl.multiple_of(i * fw, fw), fw), :] = rows_ref[
                pl.ds(pl.multiple_of(src * fw, fw), fw), :
            ]

        @pl.when(jnp.logical_and(mine, z != root))
        def _():
            remote(part(src), slot(i), z_up.at[i], z_recv.at[i], {"samp": mate}).wait_recv()

            @pl.when(jnp.logical_and(z > root, z + 1 < nf))
            def _():
                up(slot(i), i).start()

            @pl.when(jnp.logical_and(z < root, z > 0))
            def _():
                down(slot(i), i).start()

        return carry

    lax.fori_loop(0, n, exchange, 0)

    for r in range(1, n):
        for copy in small(r):
            copy.wait_send()
    for r in direct:
        own_points(r).wait_send()
        own_part(r).wait_send()
    for r in range(2, n, 2):
        src = xor(me, r, bits)
        pass_points(src).wait_send()
        pass_part(src).wait_send()
    for i in range(pieces):
        @pl.when(jnp.logical_and(z >= root, z + 1 < nf))
        def _():
            up(slot(i), i).wait_send()

        @pl.when(jnp.logical_and(z <= root, z > 0))
        def _():
            down(slot(i), i).wait_send()


def per_device(n, nf, points, frequencies, phases, signs, picks):
    rows, depth = points.shape
    width = frequencies.shape[1]
    keep = picks.shape[0]
    fw = width // n
    m = keep * n
    scale = (2.0 / float(m * rows * n)) ** 0.5
    phases = phases[None, :]
    if fw % LANES:
        at = lax.axis_index("samp") * fw
        frequencies = lax.dynamic_slice_in_dim(frequencies, at, fw, 1)
        phases = lax.dynamic_slice_in_dim(phases, at, fw, 1)
    columns = width * nf // n
    pieces = columns // fw
    vmem = pl.BlockSpec(memory_space=pltpu.VMEM)
    hbm = pl.BlockSpec(memory_space=pl.ANY)
    dma = pltpu.SemaphoreType.DMA
    block, slab = pl.pallas_call(
        functools.partial(sketch_kernel, n, nf, scale),
        out_shape=(
            jax.ShapeDtypeStruct((width, m), jnp.bfloat16),
            jax.ShapeDtypeStruct((columns, m), jnp.bfloat16),
        ),
        in_specs=[vmem, hbm, hbm, vmem, vmem],
        out_specs=(vmem, vmem),
        scratch_shapes=[
            pltpu.VMEM((n, rows, depth), jnp.bfloat16),
            pltpu.VMEM((n, 1, rows), jnp.int32),
            pltpu.VMEM((n, keep, LANES), jnp.int32),
            pltpu.VMEM((depth, fw), jnp.bfloat16),
            pltpu.VMEM((1, fw), jnp.float32),
            pltpu.VMEM((m, rows), jnp.float32),
            pltpu.VMEM((m, rows), jnp.bfloat16),
            pltpu.VMEM((m, fw), jnp.float32),
        ]
        + [dma((n,))] * 10
        + [dma((pieces,))] * 3
        + [dma((5,))],
        compiler_params=pltpu.CompilerParams(collective_id=0, has_side_effects=True),
    )(points, frequencies, phases, signs[None, :], jnp.broadcast_to(picks[:, None], (keep, LANES)))
    return lax.dot_general(
        block, slab, (((1,), (1,)), ((), ())), preferred_element_type=jnp.float32
    )


def solution(mesh):
    return jax.shard_map(
        functools.partial(per_device, mesh.shape["samp"], mesh.shape["feat"]),
        mesh=mesh,
        in_specs=(P("samp", None), P(None, "feat"), P("feat"), P("samp"), P("samp")),
        out_specs=P("feat", "samp"),
        check_vma=False,
    )
```

```python
import functools

import jax
import jax.numpy as jnp
from jax import lax
from jax.experimental import pallas as pl
from jax.experimental.pallas import tpu as pltpu
from jax.sharding import PartitionSpec as P

MESH = pl.DeviceIdType.MESH
LANES = 128
NT = (((1,), (1,)), ((), ()))
SINE = (6.283185160089389, -41.34165503139731, 81.60100407217423, -76.54978227052618, 39.53670590280816)


def xor(a, b, bits):
    return sum(((a // 2**k + b // 2**k) % 2) * 2**k for k in range(bits))


def parity(value):
    for shift in (16, 8, 4, 2, 1):
        value = jnp.bitwise_xor(value, jnp.right_shift(value, shift))
    return jnp.bitwise_and(value, 1)


def flip(value):
    return 1.0 - 2.0 * parity(value).astype(jnp.float32)


def cosine(x):
    turns = x * 0.15915494309189535
    whole = (turns + 12582912.0) - 12582912.0
    y = 0.25 - jnp.abs(turns - whole)
    w = y * y
    p = w * SINE[4] + SINE[3]
    for c in SINE[2::-1]:
        p = p * w + c
    return p * y


class Gather:
    def __init__(self, me, mate, bits, own, block, send, recv):
        self.me, self.mate, self.bits = me, mate, bits
        self.own, self.block, self.send, self.recv = own, block, send, recv
        self.routes = []

    def copy(self, r, k, to, slot):
        src = xor(self.me, r, self.bits)
        here = self.own(k) if r == 0 else self.block(src, k)
        peer = self.mate if to == 1 else xor(self.me, to, self.bits)
        return pltpu.make_async_remote_copy(
            src_ref=here, dst_ref=self.block(src, k), send_sem=self.send.at[slot],
            recv_sem=self.recv.at[src, k], device_id={"samp": peer}, device_id_type=MESH,
        )

    def push(self, r, k, to):
        slot = len(self.routes)
        self.routes.append((r, k, to, slot))
        self.copy(r, k, to, slot).start()

    def start(self):
        for k in (0, 1):
            for b in range(1, self.bits):
                self.push(0, k if b == 1 else 1 - k, 1 << b)
        for k in (0, 1):
            self.push(0, k, 1)

    def arrive(self, r):
        for k in (0, 1):
            self.copy(r, k, 1, 0).wait_recv()
            if r % 2 == 0:
                q = r // 2
                top, low = q.bit_length() - 1, (q & -q).bit_length() - 1
                onward = range(top + 1, self.bits - 1) if k == 0 else range(low)
                for b in onward:
                    self.push(r, k, 2 << b)
                self.push(r, k, 1)

    def finish(self):
        for route in self.routes:
            self.copy(*route).wait_send()


def sends(n):
    bits = n.bit_length() - 1
    count = 2 * bits
    for r in range(2, n, 2):
        q = r // 2
        count += 2 + bits - 1 - q.bit_length() + (q & -q).bit_length() - 1
    return count


def sketch_kernel(
    n, nf, scale, pts_ref, freq_ref, phase_ref, signs_ref, picks_ref, rows_ref, cols_ref,
    pts, sgn, pks, fbuf, pbuf, hloc, smat, acc, ftr, ptr, wide,
    p_send, p_recv, s_send, s_recv, k_send, k_recv,
    r_send, r_recv, z_up, z_down, z_recv, local_sem,
):
    bits = n.bit_length() - 1
    me = lax.axis_index("samp")
    z = lax.axis_index("feat")
    core = me % 2
    mate = me + 1 - 2 * core
    rows = pts_ref.shape[0]
    fw = acc.shape[0]
    m = acc.shape[1]
    ratio = n // nf
    pieces = n // ratio
    root = me // ratio
    half = me % ratio

    loads = []
    if fw % LANES == 0:
        at = pl.multiple_of(me * fw, LANES)
        loads = [
            pltpu.make_async_copy(freq_ref.at[:, pl.ds(at, fw)], fbuf, local_sem.at[0]),
            pltpu.make_async_copy(phase_ref.at[:, pl.ds(at, fw)], pbuf, local_sem.at[1]),
        ]
    else:
        loads = [
            pltpu.make_async_copy(freq_ref, fbuf, local_sem.at[0]),
            pltpu.make_async_copy(phase_ref, pbuf, local_sem.at[1]),
        ]
    loads.append(pltpu.make_async_copy(pts_ref, pts.at[me], local_sem.at[2]))
    loads.append(pltpu.make_async_copy(signs_ref, sgn.at[me], local_sem.at[3]))
    loads.append(pltpu.make_async_copy(picks_ref, pks.at[me], local_sem.at[4]))
    for load in loads:
        load.start()

    barrier = pltpu.get_barrier_semaphore()
    for r in range(1, n):
        pl.semaphore_signal(barrier, inc=1, device_id={"samp": xor(me, r, bits)}, device_id_type=MESH)

    @pl.when(z + 1 < nf)
    def _():
        pl.semaphore_signal(barrier, inc=1, device_id={"feat": z + 1}, device_id_type=MESH)

    @pl.when(z > 0)
    def _():
        pl.semaphore_signal(barrier, inc=1, device_id={"feat": z - 1}, device_id_type=MESH)

    ends = jnp.where(z > 0, 1, 0) + jnp.where(z + 1 < nf, 1, 0)
    pl.semaphore_wait(barrier, n - 1 + ends)

    def remote(src, dst, send, recv, to):
        return pltpu.make_async_remote_copy(
            src_ref=src, dst_ref=dst, send_sem=send, recv_sem=recv, device_id=to, device_id_type=MESH
        )

    def small(r):
        peer = xor(me, r, bits)
        return (
            remote(picks_ref, pks.at[me], k_send.at[r], k_recv.at[me], {"samp": peer}),
            remote(signs_ref, sgn.at[me], s_send.at[r], s_recv.at[me], {"samp": peer}),
        )

    for r in range(1, n):
        for copy in small(r):
            copy.start()

    half_width = fw // 2
    near = [1 << b for b in range(1, bits)]
    far = [r for r in range(2, n, 2) if r not in near]
    halved = rows // 2
    points = Gather(
        me, mate, bits, lambda k: pts_ref.at[pl.ds(k * halved, halved), :],
        lambda g, k: pts.at[g, pl.ds(k * halved, halved), :], p_send, p_recv,
    )
    points.start()

    for load in loads:
        load.wait()
    for r in range(1, n):
        peer = xor(me, r, bits)
        remote(picks_ref, pks.at[peer], k_send.at[r], k_recv.at[peer], {"samp": peer}).wait_recv()

    keep = picks_ref.shape[1]
    eye = lax.broadcasted_iota(jnp.int32, (keep, keep), 0) == lax.broadcasted_iota(jnp.int32, (keep, keep), 1)
    for g in range(n):
        line = jnp.broadcast_to(pks[g].astype(jnp.float32), (keep, keep))
        column = jnp.sum(jnp.where(eye, line, 0.0), axis=1, keepdims=True)
        wide[g * keep : (g + 1) * keep, :] = jnp.broadcast_to(column, (keep, LANES)).astype(jnp.int32)
    picks = wide[...]
    lane = lax.broadcasted_iota(jnp.int32, (m, LANES), 1)
    for l in range(rows // LANES):
        hloc[:, l * LANES : (l + 1) * LANES] = flip(
            jnp.bitwise_and(jnp.bitwise_and(picks, rows - 1), lane + l * LANES)
        )
    acc[...] = jnp.zeros_like(acc)

    tile = min(fw, 256)
    ftr[...] = fbuf[...].astype(jnp.float32).T.astype(jnp.bfloat16)
    ptr[...] = jnp.broadcast_to(pbuf[...], (8, fw)).T[:, :1]

    def step(r, carry):
        src = xor(me, r, bits)

        for q in range(1, n):
            @pl.when(r == q)
            def _(q=q):
                for first in near if q == 2 else [] if q in near else [q]:
                    points.arrive(first)

        @pl.when(r > 0)
        def _():
            remote(signs_ref, sgn.at[src], s_send.at[r], s_recv.at[src], {"samp": mate}).wait_recv()

        group = flip(jnp.bitwise_and(wide[...], src * rows))
        for l in range(rows // LANES):
            s = slice(l * LANES, (l + 1) * LANES)
            smat[:, s] = (hloc[:, s] * (group * sgn[src, :, s].astype(jnp.float32))).astype(jnp.bfloat16)
        for k in range(fw // tile):
            s = slice(k * tile, (k + 1) * tile)
            x = lax.dot_general(ftr[s, :], pts[src], NT, preferred_element_type=jnp.float32) + ptr[s, :]
            c = cosine(x)
            hi = c.astype(jnp.bfloat16)
            lo = (c - hi.astype(jnp.float32)).astype(jnp.bfloat16)
            acc[s, :] += lax.dot_general(hi, smat[...], NT, preferred_element_type=jnp.float32) + lax.dot_general(
                lo, smat[...], NT, preferred_element_type=jnp.float32
            )
        return carry

    lax.fori_loop(0, n, step, 0)

    def part(g, k):
        return rows_ref.at[pl.ds(pl.multiple_of(g * fw + k * half_width, half_width), half_width), :]

    def slot(i, k):
        return cols_ref.at[pl.ds(pl.multiple_of(i * fw + k * half_width, half_width), half_width), :]

    rows_ref[pl.ds(pl.multiple_of(me * fw, fw), fw), :] = (acc[...] * scale).astype(jnp.bfloat16)

    parts = Gather(me, mate, bits, lambda k: part(me, k), part, r_send, r_recv)
    parts.start()

    def up(src_ref, i, k):
        return remote(src_ref, slot(i, k), z_up.at[i, k], z_recv.at[i, k], {"feat": z + 1})

    def down(src_ref, i, k):
        return remote(src_ref, slot(i, k), z_down.at[i, k], z_recv.at[i, k], {"feat": z - 1})

    def along(r):
        src = xor(me, r, bits)
        i = src % pieces
        mine = src // pieces == half

        @pl.when(jnp.logical_and(mine, z == root))
        def _():
            @pl.when(z + 1 < nf)
            def _():
                for k in (0, 1):
                    up(part(src, k), i, k).start()

            @pl.when(z > 0)
            def _():
                for k in (0, 1):
                    down(part(src, k), i, k).start()

            cols_ref[pl.ds(pl.multiple_of(i * fw, fw), fw), :] = rows_ref[
                pl.ds(pl.multiple_of(src * fw, fw), fw), :
            ]

        @pl.when(jnp.logical_and(mine, z != root))
        def _():
            for k in (0, 1):
                remote(part(src, k), slot(i, k), z_up.at[i, k], z_recv.at[i, k], {"samp": mate}).wait_recv()

                @pl.when(jnp.logical_and(z > root, z + 1 < nf))
                def _():
                    up(slot(i, k), i, k).start()

                @pl.when(jnp.logical_and(z < root, z > 0))
                def _():
                    down(slot(i, k), i, k).start()

    parts.arrive(1)
    for r in near:
        parts.arrive(r)
    for r in [0, 1] + near:
        along(r)
    for r in near:
        parts.arrive(r + 1)
        along(r + 1)
    for r in far:
        parts.arrive(r)
        along(r)
        parts.arrive(r + 1)
        along(r + 1)

    for r in range(1, n):
        for copy in small(r):
            copy.wait_send()
    points.finish()
    parts.finish()
    for i, k in [(i, k) for i in range(pieces) for k in (0, 1)]:
        @pl.when(jnp.logical_and(z >= root, z + 1 < nf))
        def _():
            up(slot(i, k), i, k).wait_send()

        @pl.when(jnp.logical_and(z <= root, z > 0))
        def _():
            down(slot(i, k), i, k).wait_send()


def gram_kernel(a_ref, b_ref, o_ref):
    tall = min(o_ref.shape[0], 1024)
    for i in range(o_ref.shape[0] // tall):
        s = slice(i * tall, (i + 1) * tall)
        o_ref[s, :] = lax.dot_general(
            a_ref[s, :], b_ref[...], NT, preferred_element_type=jnp.float32
        )


def gram(block, slab):
    tall, m = block.shape
    wide = slab.shape[0]
    step = min(wide, 256)
    return pl.pallas_call(
        gram_kernel,
        out_shape=jax.ShapeDtypeStruct((tall, wide), jnp.float32),
        grid=(wide // step,),
        in_specs=[pl.BlockSpec((tall, m), lambda j: (0, 0)), pl.BlockSpec((step, m), lambda j: (j, 0))],
        out_specs=pl.BlockSpec((tall, step), lambda j: (0, j)),
    )(block, slab)


def per_device(n, nf, points, frequencies, phases, signs, picks):
    rows, depth = points.shape
    width = frequencies.shape[1]
    keep = picks.shape[0]
    fw = width // n
    m = keep * n
    scale = (2.0 / float(m * rows * n)) ** 0.5
    phases = phases[None, :]
    if fw % LANES:
        at = lax.axis_index("samp") * fw
        frequencies = lax.dynamic_slice_in_dim(frequencies, at, fw, 1)
        phases = lax.dynamic_slice_in_dim(phases, at, fw, 1)
    columns = width * nf // n
    pieces = columns // fw
    vmem = pl.BlockSpec(memory_space=pltpu.VMEM)
    hbm = pl.BlockSpec(memory_space=pl.ANY)
    dma = pltpu.SemaphoreType.DMA
    block, slab = pl.pallas_call(
        functools.partial(sketch_kernel, n, nf, scale),
        out_shape=(
            jax.ShapeDtypeStruct((width, m), jnp.bfloat16),
            jax.ShapeDtypeStruct((columns, m), jnp.bfloat16),
        ),
        in_specs=[vmem, hbm, hbm, vmem, vmem],
        out_specs=(vmem, vmem),
        scratch_shapes=[
            pltpu.VMEM((n, rows, depth), jnp.bfloat16),
            pltpu.VMEM((n, 1, rows), jnp.int32),
            pltpu.VMEM((n, 1, keep), jnp.int32),
            pltpu.VMEM((depth, fw), jnp.bfloat16),
            pltpu.VMEM((1, fw), jnp.float32),
            pltpu.VMEM((m, rows), jnp.float32),
            pltpu.VMEM((m, rows), jnp.bfloat16),
            pltpu.VMEM((fw, m), jnp.float32),
            pltpu.VMEM((fw, depth), jnp.bfloat16),
            pltpu.VMEM((fw, 1), jnp.float32),
            pltpu.VMEM((m, LANES), jnp.int32),
        ]
        + [dma((sends(n),)), dma((n, 2))]
        + [dma((n,))] * 4
        + [dma((sends(n),)), dma((n, 2))]
        + [dma((pieces, 2))] * 3
        + [dma((5,))],
        compiler_params=pltpu.CompilerParams(collective_id=0, has_side_effects=True),
    )(points, frequencies, phases, signs[None, :], picks[None, :])
    return gram(block, slab)


def solution(mesh):
    return jax.shard_map(
        functools.partial(per_device, mesh.shape["samp"], mesh.shape["feat"]),
        mesh=mesh,
        in_specs=(P("samp", None), P(None, "feat"), P("feat"), P("samp"), P("samp")),
        out_specs=P("feat", "samp"),
        check_vma=False,
    )
```
